32 devices in a mesh: group: 2 (over core), expert: 8 (over z, y), dp: 2 (over x).
Axes of the slice: x: 2, y: 2, z: 4, core: 2. Of those that a mesh axis runs over, the one named last changes fastest.
Arguments:
- tokens: bfloat16 [512, 5120], P(('group', 'expert'), 'dp'), may hold values from -6 to 6
- grad_out: bfloat16 [512, 5120], P(('group', 'expert'), 'dp'), may hold values from -6 to 6
- expert_ids: int32 [512, 8], replicated, may hold values from 0 to 15, as said below
- gate_score: float32 [512, 8], replicated, may hold values from -6 to 6
- w_gate_up: bfloat16 [16, 5120, 2, 1024], P(('group', 'expert'), 'dp'), may hold values from -0.078125 to 0.078125
- w_down: bfloat16 [16, 1024, 5120], P(('group', 'expert'), None, 'dp'), may hold values from -0.1875 to 0.1875
Outputs:
- layer_out: bfloat16 [512, 5120], P(('group', 'expert'), 'dp')
- grad_in: bfloat16 [512, 5120], P(('group', 'expert'), 'dp')
The draws below stay inside these ranges and needn't reach their ends.
Inputs may be any that keep to these rules, and one draw needn't show every extreme that they name: `expert_ids`: each row names 8 distinct experts, expert number = group * 8 + index, lying in exactly 1 group with 8 experts in each, listed by rising group. In every aligned block of 32 rows each group is named by exactly half of the rows. For a group g and an index e, among the rows of the blocks numbered j * 8 + e (j from 0 to 1) that name group g, no expert of g is named more than 32 times, and some expert of g exactly 32 times.
All inputs are finite; a program needn't handle non-finite values.
Results may differ from the reference program's by a relative error of at most 0.0057.
Values may be sent and summed in bfloat16 or wider, within the bound.
A program may use at most 64 MiB of HBM per device.

```python
import jax
import jax.numpy as jnp
from jax import lax

D = 5120
H = 1024
TOPK = 8
TOK_DEV = 32
EXPERTS = 16
TOKENS = 512
CAP = 32
N_GROUP = 2
N_EXPERT = 8


def block_loads(key):
    key_perm, key_steps = jax.random.split(key)
    labels = jax.random.permutation(key_perm, N_EXPERT)
    load_counts = jnp.zeros((N_EXPERT,), jnp.int32).at[labels[0]].set(CAP)
    pick_total = TOK_DEV * TOPK
    random_pairs = jax.random.randint(key_steps, (pick_total - CAP + 1, 2), 0, N_EXPERT)

    def add_one(position, counts_now):
        chosen = labels[jnp.minimum(random_pairs[position, 0], random_pairs[position, 1])]
        is_full = counts_now[chosen] >= CAP
        chosen = jnp.where(is_full, jnp.argmin(counts_now), chosen)
        return counts_now.at[chosen].add(1)
    return lax.fori_loop(0, pick_total - CAP, add_one, load_counts)


def block_experts(key):
    key_load, key_rows = jax.random.split(key)
    load_counts = block_loads(key_load)
    row_total = N_GROUP * (TOK_DEV // 2)
    per_group = TOPK * 2 // N_GROUP
    run_ends = jnp.cumsum(load_counts)
    positions = jnp.arange(row_total * per_group, dtype=jnp.int32)
    expert = jnp.sum((run_ends[None, :] <= positions[:, None]).astype(jnp.int32), axis=1)
    pick_table = expert.reshape(per_group, row_total)
    row_order = jax.random.permutation(key_rows, row_total)
    return jnp.zeros((row_total, per_group), jnp.int32).at[row_order].set(pick_table.T)


def column_visits(key):
    key_perm, key_side = jax.random.split(key)
    shuffle = jax.random.permutation(key_perm, N_GROUP)
    side_keys = jax.random.split(key_side, N_GROUP // 2)
    chosen_side = jax.vmap(jax.random.permutation, in_axes=(0, None))(side_keys, TOK_DEV) < TOK_DEV // 2
    chosen = jnp.where(chosen_side, shuffle[0::2][:, None], shuffle[1::2][:, None])
    group_range = jnp.arange(N_GROUP, dtype=jnp.int32)
    return jnp.sum((chosen[:, :, None] == group_range).astype(jnp.int32), axis=0)


def draw_expert_ids(key, part):
    key_vis, key_blocks = jax.random.split(jax.random.fold_in(key, 7))
    columns = N_GROUP * N_EXPERT
    visitors = TOK_DEV // 2
    row_total = N_GROUP * visitors
    per_group = TOPK * 2 // N_GROUP
    visits = jax.vmap(column_visits)(jax.random.split(key_vis, columns))
    experts = jax.vmap(block_experts)(jax.random.split(key_blocks, columns)).reshape(N_GROUP, N_EXPERT, row_total, per_group)
    slot_index = jnp.maximum(jnp.cumsum(visits, axis=1) - 1, 0)
    column_range = jnp.arange(columns, dtype=jnp.int32)
    source_group = column_range // N_EXPERT
    source_index = column_range % N_EXPERT
    row_index = source_group[:, None, None] * visitors + slot_index
    target_group = jnp.arange(N_GROUP, dtype=jnp.int32)[None, None, :]
    picked = experts[target_group, source_index[:, None, None], row_index]
    global_ids = target_group[..., None] * N_EXPERT + picked
    visit_order = jnp.argsort(1 - visits, axis=2, stable=True)[:, :, :N_GROUP // 2]
    visit_index = jnp.broadcast_to(visit_order[..., None], (columns, TOK_DEV, N_GROUP // 2, per_group))
    chosen = jnp.take_along_axis(global_ids, visit_index, axis=2)
    return chosen.reshape(columns * TOK_DEV, TOPK).astype(jnp.int32)


def levels(rng, shape, shards, low, largest):
    def one(axis_at, blocks):
        draws = jax.random.uniform(jax.random.fold_in(jax.random.fold_in(rng, 6), axis_at), (blocks,), jnp.float32, low / len(shards), largest / len(shards))
        return jnp.repeat(jnp.exp(draws), shape[axis_at] // blocks).reshape((-1,) + (1,) * (len(shape) - axis_at - 1))

    factor_of = one(*shards[0])
    for cut in shards[1:]:
        factor_of = factor_of * one(*cut)
    return factor_of


def noise(rng, dims, deviation, bound, shards=(), kind=jnp.bfloat16):
    gain = levels(rng, dims, shards, -0.22, 0.18) if shards else 1.0
    values = jax.random.normal(rng, dims, jnp.float32) * deviation * gain
    return jnp.minimum(jnp.maximum(values, -bound), bound).astype(kind)


def setup_inputs(seed: int = 0) -> dict:
    seeds = jax.random.split(jax.random.key(seed), 7)
    return {
        "tokens": noise(seeds[0], (TOKENS, D), 1.0, 6.0, ((0, 16), (1, 2))),
        "grad_out": noise(seeds[1], (TOKENS, D), 1.0, 6.0, ((0, 16), (1, 2))),
        "expert_ids": draw_expert_ids(jax.random.fold_in(seeds[6], 71), 0),
        "gate_score": noise(seeds[3], (TOKENS, TOPK), 1.5, 6.0, (), jnp.float32),
        "w_gate_up": noise(seeds[4], (EXPERTS, D, 2, H), D ** -0.5, 0.078125, ((0, 16), (1, 2))),
        "w_down": noise(seeds[5], (EXPERTS, H, D), H ** -0.5, 0.1875, ((0, 16), (2, 2))),
    }


def route_weights(gate_score):
    sigmoid_score = jax.nn.sigmoid(gate_score)
    return 2.5 * sigmoid_score / jnp.sum(sigmoid_score, axis=1, keepdims=True)


def reference(tokens, grad_out, expert_ids, gate_score, w_gate_up, w_down):
    weights = route_weights(gate_score)
    most_rows = N_EXPERT * CAP
    flat_gate_up = w_gate_up.reshape(EXPERTS, D, 2 * H)

    def per_expert(totals, stacked):
        acc_out, acc_grad = totals
        number, gate_up, down_proj = stacked
        names_it = expert_ids == number
        hits = jnp.sum(names_it.astype(jnp.int32), axis=1)
        row_order = jnp.argsort(1 - hits, stable=True)[:most_rows]
        is_valid = hits[row_order].astype(jnp.float32)
        route_share = jnp.sum(jnp.where(names_it, weights, 0.0), axis=1)[row_order]
        picked_rows = tokens[row_order]
        gate_both = jnp.dot(picked_rows, gate_up, preferred_element_type=jnp.float32)
        gate_pre = gate_both[:, :H]
        up_pre = gate_both[:, H:]
        hidden = (jax.nn.silu(gate_pre) * up_pre).astype(jnp.bfloat16)
        expert_out = jnp.dot(hidden, down_proj, preferred_element_type=jnp.float32).astype(jnp.bfloat16)
        cotangent = grad_out[row_order]
        hidden_grad = jnp.dot(cotangent, down_proj.T, preferred_element_type=jnp.float32) * route_share[:, None]
        sigmoid_gate = jax.nn.sigmoid(gate_pre)
        gate_grad = hidden_grad * up_pre * sigmoid_gate * (1.0 + gate_pre * (1.0 - sigmoid_gate))
        up_grad = hidden_grad * gate_pre * sigmoid_gate
        pre_grad = jnp.concatenate([gate_grad, up_grad], axis=1).astype(jnp.bfloat16)
        input_grad = jnp.dot(pre_grad, gate_up.T, preferred_element_type=jnp.float32).astype(jnp.bfloat16)
        group_of = number // N_EXPERT
        acc_out = acc_out.at[row_order, group_of].add(expert_out.astype(jnp.float32) * (route_share * is_valid)[:, None])
        acc_grad = acc_grad.at[row_order, group_of].add(input_grad.astype(jnp.float32) * is_valid[:, None])
        return (acc_out, acc_grad), None

    empty_sum = jnp.zeros((TOKENS, N_GROUP, D), jnp.float32)
    numbers = jnp.arange(EXPERTS, dtype=jnp.int32)
    (acc_out, acc_grad), _ = lax.scan(per_expert, (empty_sum, empty_sum), (numbers, flat_gate_up, w_down))
    group_out = lax.optimization_barrier(acc_out.astype(jnp.bfloat16))
    group_grad = lax.optimization_barrier(acc_grad.astype(jnp.bfloat16))
    layer_out = jnp.sum(group_out.astype(jnp.float32), axis=1).astype(jnp.bfloat16)
    grad_in = jnp.sum(group_grad.astype(jnp.float32), axis=1).astype(jnp.bfloat16)
    return layer_out, grad_in
```

```python
import jax
import jax.numpy as jnp
from jax import lax
from jax.sharding import PartitionSpec as P

HIGHEST = lax.Precision.HIGHEST


def route_weights(gate_score):
    sigmoid_score = jax.nn.sigmoid(gate_score)
    return 2.5 * sigmoid_score / jnp.sum(sigmoid_score, axis=1, keepdims=True)


def slot_matrix(marked, places):
    running = jnp.cumsum(marked.astype(jnp.int32), axis=-2) - 1
    slot_range = jnp.arange(places, dtype=jnp.int32)
    matched = marked[..., None] & (running[..., None] == slot_range)
    return jnp.moveaxis(matched, -3, -1).astype(jnp.float32)


def local_grad(gate_pre, up_pre, hidden_grad):
    sigmoid_gate = jax.nn.sigmoid(gate_pre)
    gate_grad = hidden_grad * up_pre * sigmoid_gate * (1.0 + gate_pre * (1.0 - sigmoid_gate))
    up_grad = hidden_grad * gate_pre * sigmoid_gate
    return jnp.stack([gate_grad, up_grad], axis=1).astype(jnp.bfloat16)


def across(blocks):
    return lax.all_to_all(blocks, "group", split_axis=0, concat_axis=0, tiled=True)


def within(blocks):
    return lax.all_to_all(blocks, "expert", split_axis=0, concat_axis=0, tiled=True)


def share_sum(partial_value):
    return lax.psum_scatter(partial_value, "dp", scatter_dimension=2, tiled=True)


def share_fold(shares, step_fn, start_value):
    return step_fn(start_value, lax.all_gather(shares, "dp", axis=2, tiled=True), jnp.int32(0))


def dense_device(tokens, grad_out, expert_ids, gate_score, w_gate_up, w_down):
    groups = lax.axis_size("group")
    members = lax.axis_size("expert")
    shares = lax.axis_size("dp")
    my_group = lax.axis_index("group")
    my_index = lax.axis_index("expert")
    per_column, features = tokens.shape
    visitors = per_column // groups
    arrivals = groups * visitors
    expert_rows = members * arrivals
    top_count = expert_ids.shape[1]
    weights = route_weights(gate_score)
    my_expert = my_group * members + my_index
    share = jnp.sum(jnp.where(expert_ids == my_expert, weights, 0.0), axis=1)
    token_group = (expert_ids[:, 0] // members).reshape(groups, members, per_column)
    here = token_group == my_group
    arrival_table = slot_matrix(here[..., None], visitors)[:, :, 0]
    row_share = jnp.sum(
        arrival_table * share.reshape(groups, members, 1, per_column), axis=3
    )
    row_share = jnp.transpose(row_share, (1, 0, 2)).reshape(expert_rows, 1)
    group_range = jnp.arange(groups, dtype=jnp.int32)
    visits_mine = token_group[my_group, my_index][:, None] == group_range
    leave_table = slot_matrix(visits_mine, visitors).astype(jnp.bfloat16)
    gate_weights = w_gate_up[0]
    down_weights = w_down[0]

    both = jnp.concatenate([tokens, grad_out], axis=1)
    leaving = jnp.einsum(
        "gst,tf->gsf", leave_table, both, preferred_element_type=jnp.float32
    ).astype(jnp.bfloat16)
    arrived = across(leaving).reshape(arrivals, 2 * features)
    rows_in = lax.all_gather(arrived[:, :features], "expert", axis=0, tiled=True)
    rows_grad = lax.all_gather(arrived[:, features:], "expert", axis=0, tiled=True)

    swap = [(i, (i + 1) % shares) for i in range(shares)]

    def dp_sum(value):
        total = value
        moving = value.astype(jnp.bfloat16)
        for _ in range(shares - 1):
            moving = lax.ppermute(moving, "dp", swap)
            total = total + moving.astype(jnp.float32)
        return total

    gate_both = dp_sum(
        jnp.einsum("rf,fkh->rkh", rows_in, gate_weights, preferred_element_type=jnp.float32)
    )
    grad_sum = dp_sum(
        jnp.einsum("rf,hf->rh", rows_grad, down_weights, preferred_element_type=jnp.float32)
    )
    gate_pre = gate_both[:, 0]
    up_pre = gate_both[:, 1]
    hidden = (jax.nn.silu(gate_pre) * up_pre).astype(jnp.bfloat16)
    expert_out = jnp.dot(hidden, down_weights, preferred_element_type=jnp.float32)
    out_part = (expert_out * row_share).astype(jnp.bfloat16)
    pre_grad = local_grad(gate_pre, up_pre, grad_sum * row_share)
    grad_part = jnp.einsum(
        "rkh,fkh->rf", pre_grad, gate_weights, preferred_element_type=jnp.float32
    ).astype(jnp.bfloat16)
    out_sum = lax.psum_scatter(out_part, "expert", scatter_dimension=0, tiled=True)
    grad_total = lax.psum_scatter(grad_part, "expert", scatter_dimension=0, tiled=True)

    def give_back(summed):
        home = across(summed.reshape(groups, visitors, features))
        return jnp.einsum(
            "gst,gsf->tf", leave_table, home, preferred_element_type=jnp.float32
        ).astype(jnp.bfloat16)

    return (give_back(out_sum), give_back(grad_total))


def on_device(tokens, grad_out, expert_ids, gate_score, w_gate_up, w_down):
    groups = lax.axis_size("group")
    members = lax.axis_size("expert")
    my_group = lax.axis_index("group")
    my_index = lax.axis_index("expert")
    per_column = tokens.shape[0]
    features = tokens.shape[1]
    visitors = per_column // 2
    top_count = expert_ids.shape[1]
    arrivals = groups * visitors
    capacity = min(arrivals, (3 * per_column * top_count + 2 * members - 1) // (2 * members))
    expert_rows = members * capacity
    weights = route_weights(gate_score).reshape(groups, members, per_column, top_count)
    pick_ids = expert_ids.reshape(groups, members, per_column, top_count)
    group_range = jnp.arange(groups, dtype=jnp.int32)
    my_picks = pick_ids[my_group, my_index]
    visits_mine = jnp.any(my_picks[:, :, None] // members == group_range, axis=1)
    leave_table = slot_matrix(visits_mine, visitors).astype(jnp.bfloat16)
    visits_here = jnp.any(pick_ids // members == my_group, axis=3)
    arrival_table = slot_matrix(visits_here[..., None], visitors)[:, :, 0]
    row_ids = jnp.einsum(
        "gest,getk->gesk", arrival_table, pick_ids.astype(jnp.float32), precision=HIGHEST
    )
    row_weights = jnp.einsum("gest,getk->gesk", arrival_table, weights, precision=HIGHEST)
    targets = (my_group * members + jnp.arange(members, dtype=jnp.int32)).astype(jnp.float32)
    matched = row_ids[..., None] == targets
    picked = jnp.any(matched, axis=3)
    picked_weight = jnp.sum(jnp.where(matched, row_weights[..., None], 0.0), axis=3)
    send_flags = picked[:, my_index].reshape(arrivals, members)
    send_table = slot_matrix(send_flags, capacity)
    send_share = jnp.transpose(picked_weight[:, my_index].reshape(arrivals, members))
    send_weight = send_table * send_share[:, None, :]
    came_flags = jnp.transpose(picked[:, :, :, my_index], (1, 0, 2)).reshape(members, arrivals)
    came_table = slot_matrix(came_flags[..., None], capacity)[:, 0]
    came_share = jnp.transpose(picked_weight[:, :, :, my_index], (1, 0, 2)).reshape(
        members, arrivals
    )
    slot_weight = jnp.einsum("ecr,er->ec", came_table, came_share, precision=HIGHEST).reshape(
        expert_rows
    )

    def dispatch(values):
        leaving = jnp.einsum(
            "gst,tf->gsf", leave_table, values, preferred_element_type=jnp.float32
        ).astype(jnp.bfloat16)
        arrived = across(leaving).reshape(arrivals, features)
        onward = jnp.einsum(
            "ecr,rf->ecf",
            send_table.astype(jnp.bfloat16),
            arrived,
            preferred_element_type=jnp.float32,
        ).astype(jnp.bfloat16)
        return within(onward).reshape(expert_rows, features)

    def combine(values, table):
        returned = within(values.reshape(members, capacity, features)).astype(jnp.float32)
        summed = jnp.einsum("ecr,ecf->rf", table, returned, precision=HIGHEST).astype(jnp.bfloat16)
        home = across(summed.reshape(groups, visitors, features))
        return jnp.einsum(
            "gst,gsf->tf", leave_table, home, preferred_element_type=jnp.float32
        ).astype(jnp.bfloat16)

    rows_in = dispatch(tokens)
    rows_grad = dispatch(grad_out)
    gate_weights = w_gate_up[0]
    down_weights = w_down[0]
    partial_value = jnp.einsum(
        "rf,fkh->rkh", rows_in, gate_weights, preferred_element_type=jnp.float32
    )
    grad_partial = jnp.einsum(
        "rf,hf->rh", rows_grad, down_weights, preferred_element_type=jnp.float32
    )
    empty_rows = jnp.zeros((expert_rows, features), jnp.float32)
    gate_both = share_sum(partial_value)
    gate_pre = gate_both[:, 0]
    up_pre = gate_both[:, 1]
    hidden = (jax.nn.silu(gate_pre) * up_pre).astype(jnp.bfloat16)[:, None, :]

    def down_step(running_sum, gathered, first_row):
        return jnp.dot(gathered[:, 0], down_weights, preferred_element_type=jnp.float32)

    expert_out = share_fold(hidden, down_step, empty_rows).astype(jnp.bfloat16)
    hidden_grad = share_sum(grad_partial[:, None, :])[:, 0] * slot_weight[:, None]
    pre_grad = local_grad(gate_pre, up_pre, hidden_grad)

    def input_step(running_sum, gathered, first_row):
        return jnp.einsum("rkh,fkh->rf", gathered, gate_weights, preferred_element_type=jnp.float32)

    expert_grad = share_fold(pre_grad, input_step, empty_rows).astype(jnp.bfloat16)
    layer_out = combine(expert_out, send_weight)
    grad_in = combine(expert_grad, send_table)
    return (layer_out, grad_in)


def per_device(tokens, grad_out, expert_ids, gate_score, w_gate_up, w_down):
    dense = expert_ids.shape[1] == lax.axis_size("expert")
    plan = dense_device if dense else on_device
    return plan(tokens, grad_out, expert_ids, gate_score, w_gate_up, w_down)


def solution(mesh):
    return jax.shard_map(
        per_device,
        mesh=mesh,
        in_specs=(
            P(("group", "expert"), "dp"),
            P(("group", "expert"), "dp"),
            P(),
            P(),
            P(("group", "expert"), "dp", None, None),
            P(("group", "expert"), None, "dp"),
        ),
        out_specs=(P(("group", "expert"), "dp"), P(("group", "expert"), "dp")),
        check_vma=False,
    )
```

```python
import functools

import jax
import jax.numpy as jnp
from jax import lax
from jax.experimental import pallas as pl
from jax.experimental.pallas import tpu as pltpu
from jax.sharding import PartitionSpec as P

HIGHEST = lax.Precision.HIGHEST


def route_weights(gate_score):
    sigmoid_score = jax.nn.sigmoid(gate_score)
    return 2.5 * sigmoid_score / jnp.sum(sigmoid_score, axis=1, keepdims=True)


def slot_matrix(marked, places):
    running = jnp.cumsum(marked.astype(jnp.int32), axis=-2) - 1
    slot_range = jnp.arange(places, dtype=jnp.int32)
    matched = marked[..., None] & (running[..., None] == slot_range)
    return jnp.moveaxis(matched, -3, -1).astype(jnp.float32)


def local_grad(gate_pre, up_pre, hidden_grad):
    sigmoid_gate = jax.nn.sigmoid(gate_pre)
    gate_grad = hidden_grad * up_pre * sigmoid_gate * (1.0 + gate_pre * (1.0 - sigmoid_gate))
    up_grad = hidden_grad * gate_pre * sigmoid_gate
    return jnp.stack([gate_grad, up_grad], axis=1).astype(jnp.bfloat16)


def across(blocks):
    return lax.all_to_all(blocks, "group", split_axis=0, concat_axis=0, tiled=True)


def within(blocks):
    return lax.all_to_all(blocks, "expert", split_axis=0, concat_axis=0, tiled=True)


def share_sum(partial_value):
    return lax.psum_scatter(partial_value, "dp", scatter_dimension=2, tiled=True)


def share_fold(shares, step_fn, start_value):
    return step_fn(start_value, lax.all_gather(shares, "dp", axis=2, tiled=True), jnp.int32(0))


MESH = pl.DeviceIdType.MESH
LANES = 2


def greet(groups, me, lines):
    my_group = lax.axis_index("group")
    line = me // LANES
    barrier = pltpu.get_barrier_semaphore()

    def hello(where):
        pl.semaphore_signal(barrier, inc=1, device_id=where, device_id_type=MESH)

    for step in range(1, groups):
        hello({"group": lax.rem(my_group + step, groups)})
    hello({"expert": line * LANES + 1 - lax.rem(me, LANES)})

    @pl.when(line < lines - 1)
    def _():
        hello({"expert": me + LANES})

    @pl.when(line > 0)
    def _():
        hello({"expert": me - LANES})

    ends = (line < lines - 1).astype(jnp.int32) + (line > 0).astype(jnp.int32)
    pl.semaphore_wait(barrier, groups + ends)


def gather_kernel(groups, members, leaving, out, own_sem, pair_send, pair_recv, send, recv):
    lines = members // LANES
    my_group = lax.axis_index("group")
    me = lax.axis_index("expert")
    line, lane = me // LANES, lax.rem(me, LANES)
    beside = line * LANES + 1 - lane
    greet(groups, me, lines)

    def pair_copy(step):
        other = lax.rem(my_group + step, groups)
        return pltpu.make_async_remote_copy(
            src_ref=leaving.at[other],
            dst_ref=out.at[me, my_group],
            send_sem=pair_send.at[step],
            recv_sem=pair_recv.at[step],
            device_id={"group": other},
            device_id_type=MESH,
        )

    def pair_wait(step):
        source = lax.rem(my_group + groups - step, groups)
        pltpu.make_async_remote_copy(
            src_ref=leaving.at[source],
            dst_ref=out.at[me, source],
            send_sem=pair_send.at[step],
            recv_sem=pair_recv.at[step],
            device_id={"group": source},
            device_id_type=MESH,
        ).wait_recv()

    def hop(way, block, target):
        return pltpu.make_async_remote_copy(
            src_ref=out.at[block],
            dst_ref=out.at[block],
            send_sem=send.at[way, block],
            recv_sem=recv.at[block],
            device_id={"expert": target},
            device_id_type=MESH,
        )

    for step in range(1, groups):
        pair_copy(step).start()
    own = pltpu.make_async_copy(leaving.at[my_group], out.at[me, my_group], own_sem)
    own.start()
    own.wait()
    for step in range(1, groups):
        pair_wait(step)

    def visit(act_up, act_down, act_side, arrive):
        hop_up, hop_down, hop_side = act_up, act_down, act_side
        hop_side(me)
        pl.when(line < lines - 1)(lambda: hop_up(me))
        pl.when(line > 0)(lambda: hop_down(me))
        for reach in range(1, lines):
            @pl.when(line - reach >= 0)
            def _():
                block = me - reach * LANES
                arrive(block)
                pl.when(line < lines - 1)(lambda: hop_up(block))
                hop_side(block)

            @pl.when(line + reach <= lines - 1)
            def _():
                block = me + reach * LANES
                arrive(block)
                pl.when(line > 0)(lambda: hop_down(block))
                hop_side(block)

    visit(
        lambda block: hop(0, block, me + LANES).start(),
        lambda block: hop(1, block, me - LANES).start(),
        lambda block: hop(2, block, beside).start(),
        lambda block: hop(0, block, beside).wait_recv(),
    )
    for place in range(lines):
        hop(2, place * LANES + 1 - lane, beside).wait_recv()
    visit(
        lambda block: hop(0, block, me + LANES).wait_send(),
        lambda block: hop(1, block, me - LANES).wait_send(),
        lambda block: hop(2, block, beside).wait_send(),
        lambda block: None,
    )
    for step in range(1, groups):
        pair_copy(step).wait_send()


def reduce_kernel(
    groups, members, parts, home, side, up, down, passing, total,
    pair_send, pair_recv, side_send, side_recv, line_send, up_recv, down_recv,
):
    lines = members // LANES
    my_group = lax.axis_index("group")
    me = lax.axis_index("expert")
    line, lane = me // LANES, lax.rem(me, LANES)
    beside = line * LANES + 1 - lane
    greet(groups, me, lines)

    def side_copy(place):
        return pltpu.make_async_remote_copy(
            src_ref=parts.at[place * LANES + 1 - lane],
            dst_ref=side.at[place],
            send_sem=side_send.at[place],
            recv_sem=side_recv.at[place],
            device_id={"expert": beside},
            device_id_type=MESH,
        )

    def line_copy(land, recv, place, target):
        return pltpu.make_async_remote_copy(
            src_ref=passing.at[place],
            dst_ref=land.at[place],
            send_sem=line_send.at[place],
            recv_sem=recv.at[place],
            device_id={"expert": target},
            device_id_type=MESH,
        )

    def up_copy(place):
        return line_copy(up, up_recv, place, me + LANES)

    def down_copy(place):
        return line_copy(down, down_recv, place, me - LANES)

    def far_first(above, below):
        for reach in range(lines - 1, 0, -1):
            pl.when(line + reach <= lines - 1)(functools.partial(above, line + reach))
            pl.when(line - reach >= 0)(functools.partial(below, line - reach))

    def begin(place):
        side_copy(place).start()

    far_first(begin, begin)
    begin(line)

    def pair_sum(place):
        side_copy(place).wait_recv()
        mine = parts[place * LANES + lane].astype(jnp.float32)
        return mine + side[place].astype(jnp.float32)

    def pass_on(place, land, copy_of, has_before):
        passing[place] = pair_sum(place).astype(passing.dtype)

        @pl.when(has_before)
        def _():
            copy_of(place).wait_recv()
            both = passing_f32(place) + land[place].astype(jnp.float32)
            passing[place] = both.astype(passing.dtype)

        copy_of(place).start()

    def passing_f32(place):
        mine = parts[place * LANES + lane].astype(jnp.float32)
        return mine + side[place].astype(jnp.float32)

    far_first(
        lambda place: pass_on(place, up, up_copy, line > 0),
        lambda place: pass_on(place, down, down_copy, line < lines - 1),
    )
    total[...] = pair_sum(line)

    @pl.when(line > 0)
    def _():
        up_copy(line).wait_recv()
        total[...] += up[line].astype(jnp.float32)

    @pl.when(line < lines - 1)
    def _():
        down_copy(line).wait_recv()
        total[...] += down[line].astype(jnp.float32)

    passing[line] = total[...].astype(passing.dtype)

    def pair_copy(step):
        other = lax.rem(my_group + step, groups)
        return pltpu.make_async_remote_copy(
            src_ref=passing.at[line, other],
            dst_ref=home.at[my_group],
            send_sem=pair_send.at[step],
            recv_sem=pair_recv.at[step],
            device_id={"group": other},
            device_id_type=MESH,
        )

    for step in range(1, groups):
        pair_copy(step).start()
    home[my_group] = passing[line, my_group]
    for step in range(1, groups):
        source = lax.rem(my_group + groups - step, groups)
        pltpu.make_async_remote_copy(
            src_ref=passing.at[line, source],
            dst_ref=home.at[source],
            send_sem=pair_send.at[step],
            recv_sem=pair_recv.at[step],
            device_id={"group": source},
            device_id_type=MESH,
        ).wait_recv()
        pair_copy(step).wait_send()
    far_first(
        lambda place: up_copy(place).wait_send(),
        lambda place: down_copy(place).wait_send(),
    )
    for place in range(lines):
        side_copy(place).wait_send()


def comm_cost(array, members):
    return pl.CostEstimate(
        flops=0, bytes_accessed=32 * members * array.size * 2 // 2, transcendentals=0
    )


def gather_rows(leaving, members):
    groups, visitors, features = leaving.shape
    dma = pltpu.SemaphoreType.DMA
    return pl.pallas_call(
        functools.partial(gather_kernel, groups, members),
        out_shape=jax.ShapeDtypeStruct((members, *leaving.shape), leaving.dtype),
        in_specs=[pl.BlockSpec(memory_space=pltpu.VMEM)],
        out_specs=pl.BlockSpec(memory_space=pltpu.VMEM),
        scratch_shapes=[
            dma(()), dma((groups,)), dma((groups,)), dma((3, members)), dma((members,)),
        ],
        compiler_params=pltpu.CompilerParams(collective_id=0, has_side_effects=True),
        cost_estimate=comm_cost(leaving, members),
        name="gather_rows",
    )(leaving)


def reduce_rows(parts, groups, members):
    block = (groups, parts.shape[0] // (groups * members), parts.shape[1])
    lines = members // LANES
    dma = pltpu.SemaphoreType.DMA
    slots = pltpu.VMEM((lines, *block), parts.dtype)
    return pl.pallas_call(
        functools.partial(reduce_kernel, groups, members),
        out_shape=jax.ShapeDtypeStruct(block, parts.dtype),
        in_specs=[pl.BlockSpec(memory_space=pltpu.VMEM)],
        out_specs=pl.BlockSpec(memory_space=pltpu.VMEM),
        scratch_shapes=[
            slots, slots, slots, slots, pltpu.VMEM(block, jnp.float32),
            dma((groups,)), dma((groups,)), dma((lines,)), dma((lines,)),
            dma((lines,)), dma((lines,)), dma((lines,)),
        ],
        compiler_params=pltpu.CompilerParams(collective_id=1, has_side_effects=True),
        cost_estimate=comm_cost(parts, 1),
        name="reduce_rows",
    )(parts.reshape(members, *block))


def dense_device(tokens, grad_out, expert_ids, gate_score, w_gate_up, w_down):
    groups = lax.axis_size("group")
    members = lax.axis_size("expert")
    shares = lax.axis_size("dp")
    my_group = lax.axis_index("group")
    my_index = lax.axis_index("expert")
    per_column, features = tokens.shape
    visitors = per_column // groups
    arrivals = groups * visitors
    expert_rows = members * arrivals
    top_count = expert_ids.shape[1]
    weights = route_weights(gate_score)
    my_expert = my_group * members + my_index
    share = jnp.sum(jnp.where(expert_ids == my_expert, weights, 0.0), axis=1)
    token_group = (expert_ids[:, 0] // members).reshape(groups, members, per_column)
    here = token_group == my_group
    arrival_table = slot_matrix(here[..., None], visitors)[:, :, 0]
    row_share = jnp.sum(
        arrival_table * share.reshape(groups, members, 1, per_column), axis=3
    )
    row_share = jnp.transpose(row_share, (1, 0, 2)).reshape(expert_rows, 1)
    group_range = jnp.arange(groups, dtype=jnp.int32)
    visits_mine = token_group[my_group, my_index][:, None] == group_range
    leave_table = slot_matrix(visits_mine, visitors).astype(jnp.bfloat16)
    gate_weights = w_gate_up[0]
    down_weights = w_down[0]

    def dispatch(values):
        leaving = jnp.einsum(
            "gst,tf->gsf", leave_table, values, preferred_element_type=jnp.float32
        ).astype(jnp.bfloat16)
        return gather_rows(leaving, members).reshape(expert_rows, features)

    rows_in = dispatch(tokens)
    rows_grad = dispatch(grad_out)

    swap = [(i, (i + 1) % shares) for i in range(shares)]

    def dp_sum(value):
        total = value
        moving = value.astype(jnp.bfloat16)
        for _ in range(shares - 1):
            moving = lax.ppermute(moving, "dp", swap)
            total = total + moving.astype(jnp.float32)
        return total

    gate_both = dp_sum(
        jnp.einsum("rf,fkh->rkh", rows_in, gate_weights, preferred_element_type=jnp.float32)
    )
    grad_sum = dp_sum(
        jnp.einsum("rf,hf->rh", rows_grad, down_weights, preferred_element_type=jnp.float32)
    )
    gate_pre = gate_both[:, 0]
    up_pre = gate_both[:, 1]
    hidden = (jax.nn.silu(gate_pre) * up_pre).astype(jnp.bfloat16)
    expert_out = jnp.dot(hidden, down_weights, preferred_element_type=jnp.float32)
    out_part = (expert_out * row_share).astype(jnp.bfloat16)
    pre_grad = local_grad(gate_pre, up_pre, grad_sum * row_share)
    grad_part = jnp.einsum(
        "rkh,fkh->rf", pre_grad, gate_weights, preferred_element_type=jnp.float32
    ).astype(jnp.bfloat16)

    def give_back(parts):
        home = reduce_rows(parts, groups, members)
        return jnp.einsum(
            "gst,gsf->tf", leave_table, home, preferred_element_type=jnp.float32
        ).astype(jnp.bfloat16)

    return (give_back(out_part), give_back(grad_part))


def on_device(tokens, grad_out, expert_ids, gate_score, w_gate_up, w_down):
    groups = lax.axis_size("group")
    members = lax.axis_size("expert")
    my_group = lax.axis_index("group")
    my_index = lax.axis_index("expert")
    per_column = tokens.shape[0]
    features = tokens.shape[1]
    visitors = per_column // 2
    top_count = expert_ids.shape[1]
    arrivals = groups * visitors
    capacity = min(arrivals, (3 * per_column * top_count + 2 * members - 1) // (2 * members))
    expert_rows = members * capacity
    weights = route_weights(gate_score).reshape(groups, members, per_column, top_count)
    pick_ids = expert_ids.reshape(groups, members, per_column, top_count)
    group_range = jnp.arange(groups, dtype=jnp.int32)
    my_picks = pick_ids[my_group, my_index]
    visits_mine = jnp.any(my_picks[:, :, None] // members == group_range, axis=1)
    leave_table = slot_matrix(visits_mine, visitors).astype(jnp.bfloat16)
    visits_here = jnp.any(pick_ids // members == my_group, axis=3)
    arrival_table = slot_matrix(visits_here[..., None], visitors)[:, :, 0]
    row_ids = jnp.einsum(
        "gest,getk->gesk", arrival_table, pick_ids.astype(jnp.float32), precision=HIGHEST
    )
    row_weights = jnp.einsum("gest,getk->gesk", arrival_table, weights, precision=HIGHEST)
    targets = (my_group * members + jnp.arange(members, dtype=jnp.int32)).astype(jnp.float32)
    matched = row_ids[..., None] == targets
    picked = jnp.any(matched, axis=3)
    picked_weight = jnp.sum(jnp.where(matched, row_weights[..., None], 0.0), axis=3)
    send_flags = picked[:, my_index].reshape(arrivals, members)
    send_table = slot_matrix(send_flags, capacity)
    send_share = jnp.transpose(picked_weight[:, my_index].reshape(arrivals, members))
    send_weight = send_table * send_share[:, None, :]
    came_flags = jnp.transpose(picked[:, :, :, my_index], (1, 0, 2)).reshape(members, arrivals)
    came_table = slot_matrix(came_flags[..., None], capacity)[:, 0]
    came_share = jnp.transpose(picked_weight[:, :, :, my_index], (1, 0, 2)).reshape(
        members, arrivals
    )
    slot_weight = jnp.einsum("ecr,er->ec", came_table, came_share, precision=HIGHEST).reshape(
        expert_rows
    )

    def dispatch(values):
        leaving = jnp.einsum(
            "gst,tf->gsf", leave_table, values, preferred_element_type=jnp.float32
        ).astype(jnp.bfloat16)
        arrived = across(leaving).reshape(arrivals, features)
        onward = jnp.einsum(
            "ecr,rf->ecf",
            send_table.astype(jnp.bfloat16),
            arrived,
            preferred_element_type=jnp.float32,
        ).astype(jnp.bfloat16)
        return within(onward).reshape(expert_rows, features)

    def combine(values, table):
        returned = within(values.reshape(members, capacity, features)).astype(jnp.float32)
        summed = jnp.einsum("ecr,ecf->rf", table, returned, precision=HIGHEST).astype(jnp.bfloat16)
        home = across(summed.reshape(groups, visitors, features))
        return jnp.einsum(
            "gst,gsf->tf", leave_table, home, preferred_element_type=jnp.float32
        ).astype(jnp.bfloat16)

    rows_in = dispatch(tokens)
    rows_grad = dispatch(grad_out)
    gate_weights = w_gate_up[0]
    down_weights = w_down[0]
    partial_value = jnp.einsum(
        "rf,fkh->rkh", rows_in, gate_weights, preferred_element_type=jnp.float32
    )
    grad_partial = jnp.einsum(
        "rf,hf->rh", rows_grad, down_weights, preferred_element_type=jnp.float32
    )
    empty_rows = jnp.zeros((expert_rows, features), jnp.float32)
    gate_both = share_sum(partial_value)
    gate_pre = gate_both[:, 0]
    up_pre = gate_both[:, 1]
    hidden = (jax.nn.silu(gate_pre) * up_pre).astype(jnp.bfloat16)[:, None, :]

    def down_step(running_sum, gathered, first_row):
        return jnp.dot(gathered[:, 0], down_weights, preferred_element_type=jnp.float32)

    expert_out = share_fold(hidden, down_step, empty_rows).astype(jnp.bfloat16)
    hidden_grad = share_sum(grad_partial[:, None, :])[:, 0] * slot_weight[:, None]
    pre_grad = local_grad(gate_pre, up_pre, hidden_grad)

    def input_step(running_sum, gathered, first_row):
        return jnp.einsum("rkh,fkh->rf", gathered, gate_weights, preferred_element_type=jnp.float32)

    expert_grad = share_fold(pre_grad, input_step, empty_rows).astype(jnp.bfloat16)
    layer_out = combine(expert_out, send_weight)
    grad_in = combine(expert_grad, send_table)
    return (layer_out, grad_in)


def per_device(tokens, grad_out, expert_ids, gate_score, w_gate_up, w_down):
    members = lax.axis_size("expert")
    dense = expert_ids.shape[1] == members and members % LANES == 0
    plan = dense_device if dense else on_device
    return plan(tokens, grad_out, expert_ids, gate_score, w_gate_up, w_down)


def solution(mesh):
    return jax.shard_map(
        per_device,
        mesh=mesh,
        in_specs=(
            P(("group", "expert"), "dp"),
            P(("group", "expert"), "dp"),
            P(),
            P(),
            P(("group", "expert"), "dp", None, None),
            P(("group", "expert"), None, "dp"),
        ),
        out_specs=(P(("group", "expert"), "dp"), P(("group", "expert"), "dp")),
        check_vma=False,
    )
```

```python
import functools

import jax
import jax.numpy as jnp
from jax import lax
from jax.experimental import pallas as pl
from jax.experimental.pallas import tpu as pltpu
from jax.sharding import PartitionSpec as P

HIGHEST = lax.Precision.HIGHEST


def route_weights(gate_score):
    sigmoid_score = jax.nn.sigmoid(gate_score)
    return 2.5 * sigmoid_score / jnp.sum(sigmoid_score, axis=1, keepdims=True)


def slot_matrix(marked, places):
    running = jnp.cumsum(marked.astype(jnp.int32), axis=-2) - 1
    slot_range = jnp.arange(places, dtype=jnp.int32)
    matched = marked[..., None] & (running[..., None] == slot_range)
    return jnp.moveaxis(matched, -3, -1).astype(jnp.float32)


def local_grad(gate_pre, up_pre, hidden_grad):
    sigmoid_gate = jax.nn.sigmoid(gate_pre)
    gate_grad = hidden_grad * up_pre * sigmoid_gate * (1.0 + gate_pre * (1.0 - sigmoid_gate))
    up_grad = hidden_grad * gate_pre * sigmoid_gate
    return jnp.stack([gate_grad, up_grad], axis=1).astype(jnp.bfloat16)


def across(blocks):
    return lax.all_to_all(blocks, "group", split_axis=0, concat_axis=0, tiled=True)


def within(blocks):
    return lax.all_to_all(blocks, "expert", split_axis=0, concat_axis=0, tiled=True)


def share_sum(partial_value):
    return lax.psum_scatter(partial_value, "dp", scatter_dimension=2, tiled=True)


def share_fold(shares, step_fn, start_value):
    return step_fn(start_value, lax.all_gather(shares, "dp", axis=2, tiled=True), jnp.int32(0))


MESH = pl.DeviceIdType.MESH
LANES = 2


def greet(groups, me, lines):
    my_group = lax.axis_index("group")
    line = me // LANES
    barrier = pltpu.get_barrier_semaphore()

    def hello(where):
        pl.semaphore_signal(barrier, inc=1, device_id=where, device_id_type=MESH)

    for step in range(1, groups):
        hello({"group": lax.rem(my_group + step, groups)})
    hello({"expert": line * LANES + 1 - lax.rem(me, LANES)})

    @pl.when(line < lines - 1)
    def _():
        hello({"expert": me + LANES})

    @pl.when(line > 0)
    def _():
        hello({"expert": me - LANES})

    ends = (line < lines - 1).astype(jnp.int32) + (line > 0).astype(jnp.int32)
    pl.semaphore_wait(barrier, groups + ends)


def gather_kernel(groups, members, leaving, out, own_sem, pair_send, pair_recv, send, recv):
    lines = members // LANES
    my_group = lax.axis_index("group")
    me = lax.axis_index("expert")
    line, lane = me // LANES, lax.rem(me, LANES)
    beside = line * LANES + 1 - lane
    greet(groups, me, lines)

    def pair_copy(step):
        other = lax.rem(my_group + step, groups)
        return pltpu.make_async_remote_copy(
            src_ref=leaving.at[other],
            dst_ref=out.at[me, my_group],
            send_sem=pair_send.at[step],
            recv_sem=pair_recv.at[step],
            device_id={"group": other},
            device_id_type=MESH,
        )

    def pair_wait(step):
        source = lax.rem(my_group + groups - step, groups)
        pltpu.make_async_remote_copy(
            src_ref=leaving.at[source],
            dst_ref=out.at[me, source],
            send_sem=pair_send.at[step],
            recv_sem=pair_recv.at[step],
            device_id={"group": source},
            device_id_type=MESH,
        ).wait_recv()

    def hop(way, block, piece, target):
        return pltpu.make_async_remote_copy(
            src_ref=out.at[block, piece],
            dst_ref=out.at[block, piece],
            send_sem=send.at[way, block, piece],
            recv_sem=recv.at[block, piece],
            device_id={"expert": target},
            device_id_type=MESH,
        )

    def hop_up(block, piece):
        return hop(0, block, piece, me + LANES)

    def hop_down(block, piece):
        return hop(1, block, piece, me - LANES)

    def hop_side(block, piece):
        return hop(2, block, piece, beside)

    for step in range(1, groups):
        pair_copy(step).start()
    own = pltpu.make_async_copy(leaving.at[my_group], out.at[me, my_group], own_sem)
    own.start()
    own.wait()

    def visit(reach, act, arrive):
        for step in range(groups):
            def above(block, piece):
                arrive(block, piece)
                pl.when(line > 0)(lambda: act(hop_down(block, piece)))
                act(hop_side(block, piece))

            def below(block, piece):
                arrive(block, piece)
                pl.when(line < lines - 1)(lambda: act(hop_up(block, piece)))
                act(hop_side(block, piece))

            piece = lax.rem(my_group + groups - step, groups)
            pl.when(line - reach >= 0)(functools.partial(below, me - reach * LANES, piece))
            pl.when(line + reach <= lines - 1)(
                functools.partial(above, me + reach * LANES, piece)
            )

    def visit_own(step, act):
        piece = lax.rem(my_group + groups - step, groups)
        act(hop_side(me, piece))
        pl.when(line < lines - 1)(lambda: act(hop_up(me, piece)))
        pl.when(line > 0)(lambda: act(hop_down(me, piece)))

    def begin(copy):
        copy.start()

    def sent(copy):
        copy.wait_send()

    for step in range(groups):
        if step:
            pair_wait(step)
        visit_own(step, begin)
    for reach in range(1, lines):
        visit(reach, begin, lambda block, piece: hop_side(block, piece).wait_recv())
    for place in range(lines):
        for piece in range(groups):
            hop_side(place * LANES + 1 - lane, piece).wait_recv()
    for step in range(groups):
        visit_own(step, sent)
    for reach in range(1, lines):
        visit(reach, sent, lambda block, piece: None)
    for step in range(1, groups):
        pair_copy(step).wait_send()


def reduce_kernel(
    groups, members, parts, home, side, up, down, passing, total,
    pair_send, pair_recv, side_send, side_recv, line_send, up_recv, down_recv,
):
    lines = members // LANES
    my_group = lax.axis_index("group")
    me = lax.axis_index("expert")
    line, lane = me // LANES, lax.rem(me, LANES)
    beside = line * LANES + 1 - lane
    greet(groups, me, lines)

    def side_copy(place, piece):
        return pltpu.make_async_remote_copy(
            src_ref=parts.at[place * LANES + 1 - lane, piece],
            dst_ref=side.at[place, piece],
            send_sem=side_send.at[place, piece],
            recv_sem=side_recv.at[place, piece],
            device_id={"expert": beside},
            device_id_type=MESH,
        )

    def line_copy(land, recv, place, piece, target):
        return pltpu.make_async_remote_copy(
            src_ref=passing.at[place, piece],
            dst_ref=land.at[place, piece],
            send_sem=line_send.at[place, piece],
            recv_sem=recv.at[place, piece],
            device_id={"expert": target},
            device_id_type=MESH,
        )

    def up_copy(place, piece):
        return line_copy(up, up_recv, place, piece, me + LANES)

    def down_copy(place, piece):
        return line_copy(down, down_recv, place, piece, me - LANES)

    def far_first(above, below):
        for reach in range(lines - 1, 0, -1):
            for step in range(groups):
                piece = lax.rem(my_group + 1 + step, groups)
                pl.when(line + reach <= lines - 1)(
                    functools.partial(above, line + reach, piece)
                )
                pl.when(line - reach >= 0)(functools.partial(below, line - reach, piece))

    def begin(place, piece):
        side_copy(place, piece).start()

    far_first(begin, begin)
    for step in range(groups):
        begin(line, lax.rem(my_group + 1 + step, groups))

    def pair_sum(place, piece):
        mine = parts[place * LANES + lane, piece].astype(jnp.float32)
        return mine + side[place, piece].astype(jnp.float32)

    def pass_on(land, copy_of, has_before, place, piece):
        side_copy(place, piece).wait_recv()

        @pl.when(has_before)
        def _():
            copy_of(place, piece).wait_recv()
            both = pair_sum(place, piece) + land[place, piece].astype(jnp.float32)
            passing[place, piece] = both.astype(passing.dtype)

        @pl.when(jnp.logical_not(has_before))
        def _():
            passing[place, piece] = pair_sum(place, piece).astype(passing.dtype)

        copy_of(place, piece).start()

    far_first(
        functools.partial(pass_on, up, up_copy, line > 0),
        functools.partial(pass_on, down, down_copy, line < lines - 1),
    )

    def pair_copy(step):
        other = lax.rem(my_group + step, groups)
        return pltpu.make_async_remote_copy(
            src_ref=passing.at[line, other],
            dst_ref=home.at[my_group],
            send_sem=pair_send.at[step],
            recv_sem=pair_recv.at[step],
            device_id={"group": other},
            device_id_type=MESH,
        )

    for step in range(1, groups + 1):
        piece = lax.rem(my_group + step, groups)
        side_copy(line, piece).wait_recv()
        total[...] = pair_sum(line, piece)

        @pl.when(line > 0)
        def _():
            up_copy(line, piece).wait_recv()
            total[...] += up[line, piece].astype(jnp.float32)

        @pl.when(line < lines - 1)
        def _():
            down_copy(line, piece).wait_recv()
            total[...] += down[line, piece].astype(jnp.float32)

        if step < groups:
            passing[line, piece] = total[...].astype(passing.dtype)
            pair_copy(step).start()
        else:
            home[my_group] = total[...].astype(home.dtype)
    for step in range(1, groups):
        source = lax.rem(my_group + groups - step, groups)
        pltpu.make_async_remote_copy(
            src_ref=passing.at[line, source],
            dst_ref=home.at[source],
            send_sem=pair_send.at[step],
            recv_sem=pair_recv.at[step],
            device_id={"group": source},
            device_id_type=MESH,
        ).wait_recv()
        pair_copy(step).wait_send()
    far_first(
        lambda place, piece: up_copy(place, piece).wait_send(),
        lambda place, piece: down_copy(place, piece).wait_send(),
    )
    for place in range(lines):
        for piece in range(groups):
            side_copy(place, piece).wait_send()


def comm_cost(array, members):
    return pl.CostEstimate(
        flops=0, bytes_accessed=32 * members * array.size * 2 // 2, transcendentals=0
    )


def gather_rows(leaving, members):
    groups, visitors, features = leaving.shape
    dma = pltpu.SemaphoreType.DMA
    return pl.pallas_call(
        functools.partial(gather_kernel, groups, members),
        out_shape=jax.ShapeDtypeStruct((members, *leaving.shape), leaving.dtype),
        in_specs=[pl.BlockSpec(memory_space=pltpu.VMEM)],
        out_specs=pl.BlockSpec(memory_space=pltpu.VMEM),
        scratch_shapes=[
            dma(()),
            dma((groups,)), dma((groups,)),
            dma((3, members, groups)), dma((members, groups)),
        ],
        compiler_params=pltpu.CompilerParams(
            collective_id=0, has_side_effects=True, vmem_limit_bytes=8 << 20
        ),
        cost_estimate=comm_cost(leaving, members),
        name="gather_rows",
    )(leaving)


def reduce_rows(parts, groups, members):
    block = (groups, parts.shape[0] // (groups * members), parts.shape[1])
    lines = members // LANES
    dma = pltpu.SemaphoreType.DMA
    slots = pltpu.VMEM((lines, *block), parts.dtype)
    return pl.pallas_call(
        functools.partial(reduce_kernel, groups, members),
        out_shape=jax.ShapeDtypeStruct(block, parts.dtype),
        in_specs=[pl.BlockSpec(memory_space=pltpu.VMEM)],
        out_specs=pl.BlockSpec(memory_space=pltpu.VMEM),
        scratch_shapes=[
            slots, slots, slots, slots, pltpu.VMEM(block[1:], jnp.float32),
            dma((groups,)), dma((groups,)), *[dma((lines, groups))] * 5,
        ],
        compiler_params=pltpu.CompilerParams(
            collective_id=1, has_side_effects=True, vmem_limit_bytes=12 << 20
        ),
        cost_estimate=comm_cost(parts, 1),
        name="reduce_rows",
    )(parts.reshape(members, *block))


def dense_device(tokens, grad_out, expert_ids, gate_score, w_gate_up, w_down):
    groups = lax.axis_size("group")
    members = lax.axis_size("expert")
    shares = lax.axis_size("dp")
    my_group = lax.axis_index("group")
    my_index = lax.axis_index("expert")
    per_column, features = tokens.shape
    visitors = per_column // groups
    arrivals = groups * visitors
    expert_rows = members * arrivals
    top_count = expert_ids.shape[1]
    weights = route_weights(gate_score)
    my_expert = my_group * members + my_index
    share = jnp.sum(jnp.where(expert_ids == my_expert, weights, 0.0), axis=1)
    token_group = (expert_ids[:, 0] // members).reshape(groups, members, per_column)
    here = token_group == my_group
    arrival_table = slot_matrix(here[..., None], visitors)[:, :, 0]
    row_share = jnp.sum(
        arrival_table * share.reshape(groups, members, 1, per_column), axis=3
    )
    row_share = jnp.transpose(row_share, (1, 0, 2)).reshape(expert_rows, 1)
    group_range = jnp.arange(groups, dtype=jnp.int32)
    visits_mine = token_group[my_group, my_index][:, None] == group_range
    leave_table = slot_matrix(visits_mine, visitors).astype(jnp.bfloat16)
    gate_weights = w_gate_up[0]
    down_weights = w_down[0]

    def dispatch(values):
        leaving = jnp.einsum(
            "gst,tf->gsf", leave_table, values, preferred_element_type=jnp.float32
        ).astype(jnp.bfloat16)
        return gather_rows(leaving, members).reshape(expert_rows, features)

    rows_in = dispatch(tokens)
    rows_grad = dispatch(grad_out)

    swap = [(i, (i + 1) % shares) for i in range(shares)]

    def dp_sum(value):
        total = value
        moving = value.astype(jnp.bfloat16)
        for _ in range(shares - 1):
            moving = lax.ppermute(moving, "dp", swap)
            total = total + moving.astype(jnp.float32)
        return total

    gate_both = dp_sum(
        jnp.einsum("rf,fkh->rkh", rows_in, gate_weights, preferred_element_type=jnp.float32)
    )
    grad_sum = dp_sum(
        jnp.einsum("rf,hf->rh", rows_grad, down_weights, preferred_element_type=jnp.float32)
    )
    gate_pre = gate_both[:, 0]
    up_pre = gate_both[:, 1]
    hidden = (jax.nn.silu(gate_pre) * up_pre).astype(jnp.bfloat16)
    expert_out = jnp.dot(hidden, down_weights, preferred_element_type=jnp.float32)
    out_part = (expert_out * row_share).astype(jnp.bfloat16)
    pre_grad = local_grad(gate_pre, up_pre, grad_sum * row_share)
    grad_part = jnp.einsum(
        "rkh,fkh->rf", pre_grad, gate_weights, preferred_element_type=jnp.float32
    ).astype(jnp.bfloat16)

    def give_back(parts):
        home = reduce_rows(parts, groups, members)
        return jnp.einsum(
            "gst,gsf->tf", leave_table, home, preferred_element_type=jnp.float32
        ).astype(jnp.bfloat16)

    return (give_back(out_part), give_back(grad_part))


def on_device(tokens, grad_out, expert_ids, gate_score, w_gate_up, w_down):
    groups = lax.axis_size("group")
    members = lax.axis_size("expert")
    my_group = lax.axis_index("group")
    my_index = lax.axis_index("expert")
    per_column = tokens.shape[0]
    features = tokens.shape[1]
    visitors = per_column // 2
    top_count = expert_ids.shape[1]
    arrivals = groups * visitors
    capacity = min(arrivals, (3 * per_column * top_count + 2 * members - 1) // (2 * members))
    expert_rows = members * capacity
    weights = route_weights(gate_score).reshape(groups, members, per_column, top_count)
    pick_ids = expert_ids.reshape(groups, members, per_column, top_count)
    group_range = jnp.arange(groups, dtype=jnp.int32)
    my_picks = pick_ids[my_group, my_index]
    visits_mine = jnp.any(my_picks[:, :, None] // members == group_range, axis=1)
    leave_table = slot_matrix(visits_mine, visitors).astype(jnp.bfloat16)
    visits_here = jnp.any(pick_ids // members == my_group, axis=3)
    arrival_table = slot_matrix(visits_here[..., None], visitors)[:, :, 0]
    row_ids = jnp.einsum(
        "gest,getk->gesk", arrival_table, pick_ids.astype(jnp.float32), precision=HIGHEST
    )
    row_weights = jnp.einsum("gest,getk->gesk", arrival_table, weights, precision=HIGHEST)
    targets = (my_group * members + jnp.arange(members, dtype=jnp.int32)).astype(jnp.float32)
    matched = row_ids[..., None] == targets
    picked = jnp.any(matched, axis=3)
    picked_weight = jnp.sum(jnp.where(matched, row_weights[..., None], 0.0), axis=3)
    send_flags = picked[:, my_index].reshape(arrivals, members)
    send_table = slot_matrix(send_flags, capacity)
    send_share = jnp.transpose(picked_weight[:, my_index].reshape(arrivals, members))
    send_weight = send_table * send_share[:, None, :]
    came_flags = jnp.transpose(picked[:, :, :, my_index], (1, 0, 2)).reshape(members, arrivals)
    came_table = slot_matrix(came_flags[..., None], capacity)[:, 0]
    came_share = jnp.transpose(picked_weight[:, :, :, my_index], (1, 0, 2)).reshape(
        members, arrivals
    )
    slot_weight = jnp.einsum("ecr,er->ec", came_table, came_share, precision=HIGHEST).reshape(
        expert_rows
    )

    def dispatch(values):
        leaving = jnp.einsum(
            "gst,tf->gsf", leave_table, values, preferred_element_type=jnp.float32
        ).astype(jnp.bfloat16)
        arrived = across(leaving).reshape(arrivals, features)
        onward = jnp.einsum(
            "ecr,rf->ecf",
            send_table.astype(jnp.bfloat16),
            arrived,
            preferred_element_type=jnp.float32,
        ).astype(jnp.bfloat16)
        return within(onward).reshape(expert_rows, features)

    def combine(values, table):
        returned = within(values.reshape(members, capacity, features)).astype(jnp.float32)
        summed = jnp.einsum("ecr,ecf->rf", table, returned, precision=HIGHEST).astype(jnp.bfloat16)
        home = across(summed.reshape(groups, visitors, features))
        return jnp.einsum(
            "gst,gsf->tf", leave_table, home, preferred_element_type=jnp.float32
        ).astype(jnp.bfloat16)

    rows_in = dispatch(tokens)
    rows_grad = dispatch(grad_out)
    gate_weights = w_gate_up[0]
    down_weights = w_down[0]
    partial_value = jnp.einsum(
        "rf,fkh->rkh", rows_in, gate_weights, preferred_element_type=jnp.float32
    )
    grad_partial = jnp.einsum(
        "rf,hf->rh", rows_grad, down_weights, preferred_element_type=jnp.float32
    )
    empty_rows = jnp.zeros((expert_rows, features), jnp.float32)
    gate_both = share_sum(partial_value)
    gate_pre = gate_both[:, 0]
    up_pre = gate_both[:, 1]
    hidden = (jax.nn.silu(gate_pre) * up_pre).astype(jnp.bfloat16)[:, None, :]

    def down_step(running_sum, gathered, first_row):
        return jnp.dot(gathered[:, 0], down_weights, preferred_element_type=jnp.float32)

    expert_out = share_fold(hidden, down_step, empty_rows).astype(jnp.bfloat16)
    hidden_grad = share_sum(grad_partial[:, None, :])[:, 0] * slot_weight[:, None]
    pre_grad = local_grad(gate_pre, up_pre, hidden_grad)

    def input_step(running_sum, gathered, first_row):
        return jnp.einsum("rkh,fkh->rf", gathered, gate_weights, preferred_element_type=jnp.float32)

    expert_grad = share_fold(pre_grad, input_step, empty_rows).astype(jnp.bfloat16)
    layer_out = combine(expert_out, send_weight)
    grad_in = combine(expert_grad, send_table)
    return (layer_out, grad_in)


def per_device(tokens, grad_out, expert_ids, gate_score, w_gate_up, w_down):
    members = lax.axis_size("expert")
    dense = expert_ids.shape[1] == members and members % LANES == 0
    plan = dense_device if dense else on_device
    return plan(tokens, grad_out, expert_ids, gate_score, w_gate_up, w_down)


def solution(mesh):
    return jax.shard_map(
        per_device,
        mesh=mesh,
        in_specs=(
            P(("group", "expert"), "dp"),
            P(("group", "expert"), "dp"),
            P(),
            P(),
            P(("group", "expert"), "dp", None, None),
            P(("group", "expert"), None, "dp"),
        ),
        out_specs=(P(("group", "expert"), "dp"), P(("group", "expert"), "dp")),
        check_vma=False,
    )
```

```python
import functools

import jax
import jax.numpy as jnp
from jax import lax
from jax.experimental import pallas as pl
from jax.experimental.pallas import tpu as pltpu
from jax.sharding import PartitionSpec as P

HIGHEST = lax.Precision.HIGHEST


def route_weights(gate_score):
    sigmoid_score = jax.nn.sigmoid(gate_score)
    return 2.5 * sigmoid_score / jnp.sum(sigmoid_score, axis=1, keepdims=True)


def slot_matrix(marked, places):
    running = jnp.cumsum(marked.astype(jnp.int32), axis=-2) - 1
    slot_range = jnp.arange(places, dtype=jnp.int32)
    matched = marked[..., None] & (running[..., None] == slot_range)
    return jnp.moveaxis(matched, -3, -1).astype(jnp.float32)


def local_grad(gate_pre, up_pre, hidden_grad):
    sigmoid_gate = jax.nn.sigmoid(gate_pre)
    gate_grad = hidden_grad * up_pre * sigmoid_gate * (1.0 + gate_pre * (1.0 - sigmoid_gate))
    up_grad = hidden_grad * gate_pre * sigmoid_gate
    return jnp.stack([gate_grad, up_grad], axis=1).astype(jnp.bfloat16)


def across(blocks):
    return lax.all_to_all(blocks, "group", split_axis=0, concat_axis=0, tiled=True)


def within(blocks):
    return lax.all_to_all(blocks, "expert", split_axis=0, concat_axis=0, tiled=True)


def share_sum(partial_value):
    return lax.psum_scatter(partial_value, "dp", scatter_dimension=2, tiled=True)


def share_fold(shares, step_fn, start_value):
    return step_fn(start_value, lax.all_gather(shares, "dp", axis=2, tiled=True), jnp.int32(0))


MESH = pl.DeviceIdType.MESH
LANES = 2
CUTS = 2


def greet(groups, me, lines):
    my_group = lax.axis_index("group")
    line = me // LANES
    barrier = pltpu.get_barrier_semaphore()

    def hello(where):
        pl.semaphore_signal(barrier, inc=1, device_id=where, device_id_type=MESH)

    for step in range(1, groups):
        hello({"group": lax.rem(my_group + step, groups)})
    hello({"expert": line * LANES + 1 - lax.rem(me, LANES)})

    @pl.when(line < lines - 1)
    def _():
        hello({"expert": me + LANES})

    @pl.when(line > 0)
    def _():
        hello({"expert": me - LANES})

    ends = (line < lines - 1).astype(jnp.int32) + (line > 0).astype(jnp.int32)
    pl.semaphore_wait(barrier, groups + ends)


def gather_kernel(groups, members, leaving, out, own_sem, pair_send, pair_recv, send, recv):
    lines = members // LANES
    my_group = lax.axis_index("group")
    me = lax.axis_index("expert")
    line, lane = me // LANES, lax.rem(me, LANES)
    beside = line * LANES + 1 - lane
    greet(groups, me, lines)

    def pair_copy(step, cut):
        other = lax.rem(my_group + step, groups)
        return pltpu.make_async_remote_copy(
            src_ref=leaving.at[other * CUTS + cut],
            dst_ref=out.at[me, my_group * CUTS + cut],
            send_sem=pair_send.at[step, cut],
            recv_sem=pair_recv.at[step, cut],
            device_id={"group": other},
            device_id_type=MESH,
        )

    def pair_wait(step, cut):
        source = lax.rem(my_group + groups - step, groups)
        pltpu.make_async_remote_copy(
            src_ref=leaving.at[source * CUTS + cut],
            dst_ref=out.at[me, source * CUTS + cut],
            send_sem=pair_send.at[step, cut],
            recv_sem=pair_recv.at[step, cut],
            device_id={"group": source},
            device_id_type=MESH,
        ).wait_recv()

    def hop(way, block, piece, target):
        return pltpu.make_async_remote_copy(
            src_ref=out.at[block, piece],
            dst_ref=out.at[block, piece],
            send_sem=send.at[way, block, piece],
            recv_sem=recv.at[block, piece],
            device_id={"expert": target},
            device_id_type=MESH,
        )

    def hop_up(block, piece):
        return hop(0, block, piece, me + LANES)

    def hop_down(block, piece):
        return hop(1, block, piece, me - LANES)

    def hop_side(block, piece):
        return hop(2, block, piece, beside)

    steps = [(step, cut) for step in range(groups) for cut in range(CUTS)]
    away = steps[CUTS:]
    for step, cut in away:
        pair_copy(step, cut).start()
    stay = pl.ds(my_group * CUTS, CUTS)
    own = pltpu.make_async_copy(leaving.at[stay], out.at[me, stay], own_sem)
    own.start()
    own.wait()

    def visit(reach, act, arrive):
        for step, cut in steps:
            def above(block, piece):
                arrive(block, piece)
                pl.when(line > 0)(lambda: act(hop_down(block, piece)))
                act(hop_side(block, piece))

            def below(block, piece):
                arrive(block, piece)
                pl.when(line < lines - 1)(lambda: act(hop_up(block, piece)))
                act(hop_side(block, piece))

            piece = lax.rem(my_group + groups - step, groups) * CUTS + cut
            pl.when(line - reach >= 0)(functools.partial(below, me - reach * LANES, piece))
            pl.when(line + reach <= lines - 1)(
                functools.partial(above, me + reach * LANES, piece)
            )

    def visit_own(step, cut, act):
        piece = lax.rem(my_group + groups - step, groups) * CUTS + cut
        act(hop_side(me, piece))
        pl.when(line < lines - 1)(lambda: act(hop_up(me, piece)))
        pl.when(line > 0)(lambda: act(hop_down(me, piece)))

    def begin(copy):
        copy.start()

    def sent(copy):
        copy.wait_send()

    for step, cut in steps:
        if step:
            pair_wait(step, cut)
        visit_own(step, cut, begin)
    for reach in range(1, lines):
        visit(reach, begin, lambda block, piece: hop_side(block, piece).wait_recv())
    for place in range(lines):
        for piece in range(groups * CUTS):
            hop_side(place * LANES + 1 - lane, piece).wait_recv()
    for step, cut in steps:
        visit_own(step, cut, sent)
    for reach in range(1, lines):
        visit(reach, sent, lambda block, piece: None)
    for step, cut in away:
        pair_copy(step, cut).wait_send()


def reduce_kernel(
    groups, members, parts, home, side, up, down, passing, total,
    pair_send, pair_recv, side_send, side_recv, line_send, up_recv, down_recv,
):
    lines = members // LANES
    my_group = lax.axis_index("group")
    me = lax.axis_index("expert")
    line, lane = me // LANES, lax.rem(me, LANES)
    beside = line * LANES + 1 - lane
    greet(groups, me, lines)

    def side_copy(place, piece):
        return pltpu.make_async_remote_copy(
            src_ref=parts.at[place * LANES + 1 - lane, piece],
            dst_ref=side.at[place, piece],
            send_sem=side_send.at[place, piece],
            recv_sem=side_recv.at[place, piece],
            device_id={"expert": beside},
            device_id_type=MESH,
        )

    def line_copy(land, recv, place, piece, target):
        return pltpu.make_async_remote_copy(
            src_ref=passing.at[place, piece],
            dst_ref=land.at[place, piece],
            send_sem=line_send.at[place, piece],
            recv_sem=recv.at[place, piece],
            device_id={"expert": target},
            device_id_type=MESH,
        )

    def up_copy(place, piece):
        return line_copy(up, up_recv, place, piece, me + LANES)

    def down_copy(place, piece):
        return line_copy(down, down_recv, place, piece, me - LANES)

    steps = [(step, cut) for step in range(1, groups + 1) for cut in range(CUTS)]
    away = steps[:-CUTS]

    def far_first(above, below):
        for reach in range(lines - 1, 0, -1):
            for step, cut in steps:
                piece = lax.rem(my_group + step, groups) * CUTS + cut
                pl.when(line + reach <= lines - 1)(
                    functools.partial(above, line + reach, piece)
                )
                pl.when(line - reach >= 0)(functools.partial(below, line - reach, piece))

    def begin(place, piece):
        side_copy(place, piece).start()

    far_first(begin, begin)
    for step, cut in steps:
        begin(line, lax.rem(my_group + step, groups) * CUTS + cut)

    def pair_sum(place, piece):
        mine = parts[place * LANES + lane, piece].astype(jnp.float32)
        return mine + side[place, piece].astype(jnp.float32)

    def pass_on(land, copy_of, has_before, place, piece):
        side_copy(place, piece).wait_recv()

        @pl.when(has_before)
        def _():
            copy_of(place, piece).wait_recv()
            both = pair_sum(place, piece) + land[place, piece].astype(jnp.float32)
            passing[place, piece] = both.astype(passing.dtype)

        @pl.when(jnp.logical_not(has_before))
        def _():
            passing[place, piece] = pair_sum(place, piece).astype(passing.dtype)

        copy_of(place, piece).start()

    far_first(
        functools.partial(pass_on, up, up_copy, line > 0),
        functools.partial(pass_on, down, down_copy, line < lines - 1),
    )

    def pair_copy(step, cut):
        other = lax.rem(my_group + step, groups)
        return pltpu.make_async_remote_copy(
            src_ref=passing.at[line, other * CUTS + cut],
            dst_ref=home.at[my_group * CUTS + cut],
            send_sem=pair_send.at[step, cut],
            recv_sem=pair_recv.at[step, cut],
            device_id={"group": other},
            device_id_type=MESH,
        )

    for step, cut in steps:
        piece = lax.rem(my_group + step, groups) * CUTS + cut
        side_copy(line, piece).wait_recv()
        total[...] = pair_sum(line, piece)

        @pl.when(line > 0)
        def _():
            up_copy(line, piece).wait_recv()
            total[...] += up[line, piece].astype(jnp.float32)

        @pl.when(line < lines - 1)
        def _():
            down_copy(line, piece).wait_recv()
            total[...] += down[line, piece].astype(jnp.float32)

        if step < groups:
            passing[line, piece] = total[...].astype(passing.dtype)
            pair_copy(step, cut).start()
        else:
            home[my_group * CUTS + cut] = total[...].astype(home.dtype)
    for step, cut in away:
        source = lax.rem(my_group + groups - step, groups)
        pltpu.make_async_remote_copy(
            src_ref=passing.at[line, source * CUTS + cut],
            dst_ref=home.at[source * CUTS + cut],
            send_sem=pair_send.at[step, cut],
            recv_sem=pair_recv.at[step, cut],
            device_id={"group": source},
            device_id_type=MESH,
        ).wait_recv()
        pair_copy(step, cut).wait_send()
    far_first(
        lambda place, piece: up_copy(place, piece).wait_send(),
        lambda place, piece: down_copy(place, piece).wait_send(),
    )
    for place in range(lines):
        for piece in range(groups * CUTS):
            side_copy(place, piece).wait_send()


def comm_cost(array, members):
    return pl.CostEstimate(
        flops=0, bytes_accessed=32 * members * array.size * 2 // 2, transcendentals=0
    )


def gather_rows(leaving, members):
    groups, visitors, features = leaving.shape
    leaving = leaving.reshape(groups * CUTS, visitors // CUTS, features)
    dma = pltpu.SemaphoreType.DMA
    return pl.pallas_call(
        functools.partial(gather_kernel, groups, members),
        out_shape=jax.ShapeDtypeStruct((members, *leaving.shape), leaving.dtype),
        in_specs=[pl.BlockSpec(memory_space=pltpu.VMEM)],
        out_specs=pl.BlockSpec(memory_space=pltpu.VMEM),
        scratch_shapes=[
            dma(()),
            dma((groups, CUTS)), dma((groups, CUTS)),
            dma((3, members, groups * CUTS)), dma((members, groups * CUTS)),
        ],
        compiler_params=pltpu.CompilerParams(
            collective_id=0, has_side_effects=True, vmem_limit_bytes=8 << 20
        ),
        cost_estimate=comm_cost(leaving, members),
        name="gather_rows",
    )(leaving)


def reduce_rows(parts, groups, members):
    pieces = groups * CUTS
    block = (pieces, parts.shape[0] // (pieces * members), parts.shape[1])
    lines = members // LANES
    dma = pltpu.SemaphoreType.DMA
    slots = pltpu.VMEM((lines, *block), parts.dtype)
    return pl.pallas_call(
        functools.partial(reduce_kernel, groups, members),
        out_shape=jax.ShapeDtypeStruct(block, parts.dtype),
        in_specs=[pl.BlockSpec(memory_space=pltpu.VMEM)],
        out_specs=pl.BlockSpec(memory_space=pltpu.VMEM),
        scratch_shapes=[
            slots, slots, slots, slots, pltpu.VMEM(block[1:], jnp.float32),
            dma((groups, CUTS)), dma((groups, CUTS)), *[dma((lines, pieces))] * 5,
        ],
        compiler_params=pltpu.CompilerParams(
            collective_id=1, has_side_effects=True, vmem_limit_bytes=12 << 20
        ),
        cost_estimate=comm_cost(parts, 1),
        name="reduce_rows",
    )(parts.reshape(members, *block))


def dense_device(tokens, grad_out, expert_ids, gate_score, w_gate_up, w_down):
    groups = lax.axis_size("group")
    members = lax.axis_size("expert")
    shares = lax.axis_size("dp")
    my_group = lax.axis_index("group")
    my_index = lax.axis_index("expert")
    per_column, features = tokens.shape
    visitors = per_column // groups
    arrivals = groups * visitors
    expert_rows = members * arrivals
    top_count = expert_ids.shape[1]
    weights = route_weights(gate_score)
    my_expert = my_group * members + my_index
    share = jnp.sum(jnp.where(expert_ids == my_expert, weights, 0.0), axis=1)
    token_group = (expert_ids[:, 0] // members).reshape(groups, members, per_column)
    here = token_group == my_group
    arrival_table = slot_matrix(here[..., None], visitors)[:, :, 0]
    row_share = jnp.sum(
        arrival_table * share.reshape(groups, members, 1, per_column), axis=3
    )
    row_share = jnp.transpose(row_share, (1, 0, 2)).reshape(expert_rows, 1)
    group_range = jnp.arange(groups, dtype=jnp.int32)
    visits_mine = token_group[my_group, my_index][:, None] == group_range
    leave_table = slot_matrix(visits_mine, visitors).astype(jnp.bfloat16)
    gate_weights = w_gate_up[0]
    down_weights = w_down[0]

    def dispatch(values):
        leaving = jnp.einsum(
            "gst,tf->gsf", leave_table, values, preferred_element_type=jnp.float32
        ).astype(jnp.bfloat16)
        return gather_rows(leaving, members).reshape(expert_rows, features)

    rows_in = dispatch(tokens)
    rows_grad = dispatch(grad_out)

    swap = [(i, (i + 1) % shares) for i in range(shares)]

    def dp_sum(value):
        total = value
        moving = value.astype(jnp.bfloat16)
        for _ in range(shares - 1):
            moving = lax.ppermute(moving, "dp", swap)
            total = total + moving.astype(jnp.float32)
        return total

    gate_both = dp_sum(
        jnp.einsum("rf,fkh->rkh", rows_in, gate_weights, preferred_element_type=jnp.float32)
    )
    grad_sum = dp_sum(
        jnp.einsum("rf,hf->rh", rows_grad, down_weights, preferred_element_type=jnp.float32)
    )
    gate_pre = gate_both[:, 0]
    up_pre = gate_both[:, 1]
    hidden = (jax.nn.silu(gate_pre) * up_pre).astype(jnp.bfloat16)
    expert_out = jnp.dot(hidden, down_weights, preferred_element_type=jnp.float32)
    out_part = (expert_out * row_share).astype(jnp.bfloat16)
    pre_grad = local_grad(gate_pre, up_pre, grad_sum * row_share)
    grad_part = jnp.einsum(
        "rkh,fkh->rf", pre_grad, gate_weights, preferred_element_type=jnp.float32
    ).astype(jnp.bfloat16)

    def give_back(parts):
        home = reduce_rows(parts, groups, members).reshape(groups, visitors, features)
        return jnp.einsum(
            "gst,gsf->tf", leave_table, home, preferred_element_type=jnp.float32
        ).astype(jnp.bfloat16)

    return (give_back(out_part), give_back(grad_part))


def on_device(tokens, grad_out, expert_ids, gate_score, w_gate_up, w_down):
    groups = lax.axis_size("group")
    members = lax.axis_size("expert")
    my_group = lax.axis_index("group")
    my_index = lax.axis_index("expert")
    per_column = tokens.shape[0]
    features = tokens.shape[1]
    visitors = per_column // 2
    top_count = expert_ids.shape[1]
    arrivals = groups * visitors
    capacity = min(arrivals, (3 * per_column * top_count + 2 * members - 1) // (2 * members))
    expert_rows = members * capacity
    weights = route_weights(gate_score).reshape(groups, members, per_column, top_count)
    pick_ids = expert_ids.reshape(groups, members, per_column, top_count)
    group_range = jnp.arange(groups, dtype=jnp.int32)
    my_picks = pick_ids[my_group, my_index]
    visits_mine = jnp.any(my_picks[:, :, None] // members == group_range, axis=1)
    leave_table = slot_matrix(visits_mine, visitors).astype(jnp.bfloat16)
    visits_here = jnp.any(pick_ids // members == my_group, axis=3)
    arrival_table = slot_matrix(visits_here[..., None], visitors)[:, :, 0]
    row_ids = jnp.einsum(
        "gest,getk->gesk", arrival_table, pick_ids.astype(jnp.float32), precision=HIGHEST
    )
    row_weights = jnp.einsum("gest,getk->gesk", arrival_table, weights, precision=HIGHEST)
    targets = (my_group * members + jnp.arange(members, dtype=jnp.int32)).astype(jnp.float32)
    matched = row_ids[..., None] == targets
    picked = jnp.any(matched, axis=3)
    picked_weight = jnp.sum(jnp.where(matched, row_weights[..., None], 0.0), axis=3)
    send_flags = picked[:, my_index].reshape(arrivals, members)
    send_table = slot_matrix(send_flags, capacity)
    send_share = jnp.transpose(picked_weight[:, my_index].reshape(arrivals, members))
    send_weight = send_table * send_share[:, None, :]
    came_flags = jnp.transpose(picked[:, :, :, my_index], (1, 0, 2)).reshape(members, arrivals)
    came_table = slot_matrix(came_flags[..., None], capacity)[:, 0]
    came_share = jnp.transpose(picked_weight[:, :, :, my_index], (1, 0, 2)).reshape(
        members, arrivals
    )
    slot_weight = jnp.einsum("ecr,er->ec", came_table, came_share, precision=HIGHEST).reshape(
        expert_rows
    )

    def dispatch(values):
        leaving = jnp.einsum(
            "gst,tf->gsf", leave_table, values, preferred_element_type=jnp.float32
        ).astype(jnp.bfloat16)
        arrived = across(leaving).reshape(arrivals, features)
        onward = jnp.einsum(
            "ecr,rf->ecf",
            send_table.astype(jnp.bfloat16),
            arrived,
            preferred_element_type=jnp.float32,
        ).astype(jnp.bfloat16)
        return within(onward).reshape(expert_rows, features)

    def combine(values, table):
        returned = within(values.reshape(members, capacity, features)).astype(jnp.float32)
        summed = jnp.einsum("ecr,ecf->rf", table, returned, precision=HIGHEST).astype(jnp.bfloat16)
        home = across(summed.reshape(groups, visitors, features))
        return jnp.einsum(
            "gst,gsf->tf", leave_table, home, preferred_element_type=jnp.float32
        ).astype(jnp.bfloat16)

    rows_in = dispatch(tokens)
    rows_grad = dispatch(grad_out)
    gate_weights = w_gate_up[0]
    down_weights = w_down[0]
    partial_value = jnp.einsum(
        "rf,fkh->rkh", rows_in, gate_weights, preferred_element_type=jnp.float32
    )
    grad_partial = jnp.einsum(
        "rf,hf->rh", rows_grad, down_weights, preferred_element_type=jnp.float32
    )
    empty_rows = jnp.zeros((expert_rows, features), jnp.float32)
    gate_both = share_sum(partial_value)
    gate_pre = gate_both[:, 0]
    up_pre = gate_both[:, 1]
    hidden = (jax.nn.silu(gate_pre) * up_pre).astype(jnp.bfloat16)[:, None, :]

    def down_step(running_sum, gathered, first_row):
        return jnp.dot(gathered[:, 0], down_weights, preferred_element_type=jnp.float32)

    expert_out = share_fold(hidden, down_step, empty_rows).astype(jnp.bfloat16)
    hidden_grad = share_sum(grad_partial[:, None, :])[:, 0] * slot_weight[:, None]
    pre_grad = local_grad(gate_pre, up_pre, hidden_grad)

    def input_step(running_sum, gathered, first_row):
        return jnp.einsum("rkh,fkh->rf", gathered, gate_weights, preferred_element_type=jnp.float32)

    expert_grad = share_fold(pre_grad, input_step, empty_rows).astype(jnp.bfloat16)
    layer_out = combine(expert_out, send_weight)
    grad_in = combine(expert_grad, send_table)
    return (layer_out, grad_in)


def per_device(tokens, grad_out, expert_ids, gate_score, w_gate_up, w_down):
    members = lax.axis_size("expert")
    dense = expert_ids.shape[1] == members and members % LANES == 0
    plan = dense_device if dense else on_device
    return plan(tokens, grad_out, expert_ids, gate_score, w_gate_up, w_down)


def solution(mesh):
    return jax.shard_map(
        per_device,
        mesh=mesh,
        in_specs=(
            P(("group", "expert"), "dp"),
            P(("group", "expert"), "dp"),
            P(),
            P(),
            P(("group", "expert"), "dp", None, None),
            P(("group", "expert"), None, "dp"),
        ),
        out_specs=(P(("group", "expert"), "dp"), P(("group", "expert"), "dp")),
        check_vma=False,
    )
```
